128 devices in a mesh: grp: 16 (over z, y), cand: 8 (over x, core).
Axes of the slice: x: 4, y: 4, z: 4, core: 2. Of those that a mesh axis runs over, the one named last changes fastest.
Arguments:
- history: bfloat16 [128, 1024, 256], P(('grp', 'cand')), may hold values from -9 to 9
- lengths: int32 [128], P(('grp', 'cand')), may hold values from 128 to 1024
- target: bfloat16 [128, 64, 256], P('grp', 'cand'), may hold values from -6 to 6
- bag_ids: int32 [128, 64, 32, 4], P('grp', 'cand'), may hold values from 0 to 32767
- leaf_ids: int32 [128, 64, 64], P('grp', 'cand'), may hold values from 0 to 31
- table_piece: bfloat16 [128, 8192, 128], P(('grp', 'cand')), may hold values from -6 to 6
- leaf_table: bfloat16 [64, 32, 256], replicated, may hold values from -0.75 to 0.75
- w_query: bfloat16 [256, 128], replicated, may hold values from -0.375 to 0.375
- w_key: bfloat16 [256, 128], replicated, may hold values from -0.375 to 0.375
- w_pair: bfloat16 [256, 128], replicated, may hold values from -0.375 to 0.375
- a_out: bfloat16 [128], replicated, may hold values from -1 to 1
- w_first: bfloat16 [4864, 1024], replicated, may hold values from -0.078125 to 0.078125
- w_second: bfloat16 [1024, 512], replicated, may hold values from -0.25 to 0.25
- w_third: bfloat16 [512, 256], replicated, may hold values from -0.375 to 0.375
- w_out: bfloat16 [256], replicated, may hold values from -0.5 to 0.5
Outputs:
- logits: float32 [128, 64], P('grp', 'cand')
The draws below stay inside these ranges and needn't reach their ends.
All inputs are finite; a program needn't handle non-finite values.
Results may differ from the reference program's by a relative error of at most 0.0092.
Values may be sent and summed in bfloat16 or wider, within the bound.
A program may use at most 128 MiB of HBM per device.

```python
import math
import jax
import jax.numpy as jnp
import numpy as np
from jax import lax

E = 256
HIST = 1024
ATT = 128
EMB = 128
BAG = 4
TREES = 64
LEAVES = 32
SPLIT = 4
PIECE_ROWS = 8192
HID1 = 1024
HID2 = 512
HID3 = 256
TABLES = 32
VOCAB = 32768
REQS = 128
CPR = 64
IN_WIDTH = 4864
DEVICES = 128


def draw_history(key, part):
    key_base = jax.random.fold_in(key, 11)
    key_scale = jax.random.fold_in(key, 12)
    key_shared = jax.random.fold_in(key, 13)
    base = jnp.clip(jax.random.normal(key_base, (REQS, HIST, E), jnp.float32), -3.5, 3.5)
    event_scale = jnp.exp(jax.random.uniform(key_scale, (REQS, HIST, 1), jnp.float32, -1.0, 0.7))
    shared = 0.3 * jnp.clip(jax.random.normal(key_shared, (REQS, 1, E), jnp.float32), -3.0, 3.0)
    values = jnp.clip(base * event_scale + shared, -9.0, 9.0)
    return values.astype(jnp.bfloat16)


def draw_a_out(key, part):
    key_sign = jax.random.fold_in(key, 21)
    key_size = jax.random.fold_in(key, 22)
    signs = jnp.where(jax.random.bernoulli(key_sign, 0.5, (ATT,)), 1.0, -1.0).astype(jnp.float32)
    magnitude = jax.random.uniform(key_size, (ATT,), jnp.float32, 0.75, 1.25)
    values = signs * magnitude * float(ATT) ** (-0.5)
    return values.astype(jnp.bfloat16)


def touch_ends(result, stream_key, low, largest):
    longest = result.shape.index(max(result.shape))
    spots = []
    for shift in (0, 1):
        where = [jax.random.randint(jax.random.fold_in(stream_key, axis), (), 0, length) for axis, length in enumerate(result.shape)]
        where[longest] = (where[longest] + shift) % result.shape[longest]
        spots.append(tuple(where))
    return result.at[spots[0]].set(low).at[spots[1]].set(largest)


def block_levels(key, extent, pieces, smallest, top_value):
    gain = 1.0
    for axis_at, blocks in pieces:
        heights = jax.random.uniform(jax.random.fold_in(jax.random.fold_in(key, 6), axis_at), (blocks,), jnp.float32, smallest / len(pieces), top_value / len(pieces))
        gain = gain * jnp.repeat(jnp.exp(heights), extent[axis_at] // blocks).reshape((-1,) + (1,) * (len(extent) - 1 - axis_at))
    return gain


def cumulative_ranks(count, skew):
    loads = [(1 << 20) // math.isqrt(grade ** skew) + 1 for grade in range(1, count + 1)]
    deviation = 1 + sum(loads) // (1 << 30)
    return np.cumsum(np.array([max(1, weight // deviation) for weight in loads]))


def ranked_ids(rng, extent, amount, skew):
    listing = cumulative_ranks(amount, skew)
    pick = jax.random.randint(jax.random.fold_in(rng, 1), extent, 0, int(listing[amount - 1]))
    grade = jnp.searchsorted(jnp.asarray(listing, jnp.int32), pick, side="right")
    return jax.random.permutation(jax.random.fold_in(rng, 2), amount)[grade].astype(jnp.int32)


def noise(own_key, dims, scale, most, pieces=(), kind=jnp.bfloat16):
    entries = jax.random.normal(own_key, dims, jnp.float32) * scale
    if len(pieces) > 0:
        entries = block_levels(own_key, dims, pieces, -0.22, 0.18) * entries
    return jnp.clip(entries, min=-most, max=most).astype(kind)


def setup_inputs(seed: int = 0) -> dict:
    seeds = jax.random.split(jax.random.key(seed), 16)
    history = draw_history(jax.random.fold_in(seeds[15], 71), 0)
    lengths = touch_ends(jax.random.randint(seeds[1], (REQS,), HIST // 8, HIST + 1), jax.random.fold_in(seeds[1], 1), HIST // 8, HIST).astype(jnp.int32)
    target = noise(seeds[2], (REQS, CPR, E), 1.0, 6.0, ((0, 16), (1, 8)))
    bag_ids = touch_ends(ranked_ids(seeds[3], (REQS, CPR, TABLES, BAG), VOCAB, 2), jax.random.fold_in(seeds[3], 3), 0, VOCAB - 1).astype(jnp.int32)
    leaf_ids = touch_ends(jax.random.randint(seeds[4], (REQS, CPR, TREES), 0, LEAVES), jax.random.fold_in(seeds[4], 1), 0, LEAVES - 1).astype(jnp.int32)
    table_piece = noise(seeds[5], (DEVICES, PIECE_ROWS, EMB), 1.0, 6.0, ((0, 128),))
    leaf_table = noise(seeds[6], (TREES, LEAVES, E), 0.125, 0.75)
    w_query = noise(seeds[7], (E, ATT), E ** -0.5, 0.375)
    w_key = noise(seeds[8], (E, ATT), E ** -0.5, 0.375)
    w_pair = noise(seeds[9], (E, ATT), E ** -0.5, 0.375)
    a_out = draw_a_out(jax.random.fold_in(seeds[15], 71), 0)
    w_first = noise(seeds[11], (IN_WIDTH, HID1), IN_WIDTH ** -0.5, 0.078125)
    w_second = noise(seeds[12], (HID1, HID2), (HID1 // 2) ** -0.5, 0.25)
    w_third = noise(seeds[13], (HID2, HID3), (HID2 // 2) ** -0.5, 0.375)
    w_out = noise(seeds[14], (HID3,), (HID3 // 2) ** -0.5, 0.5)
    return {"history": history, "lengths": lengths, "target": target, "bag_ids": bag_ids, "leaf_ids": leaf_ids, "table_piece": table_piece, "leaf_table": leaf_table, "w_query": w_query, "w_key": w_key, "w_pair": w_pair, "a_out": a_out, "w_first": w_first, "w_second": w_second, "w_third": w_third, "w_out": w_out}


def matmul(left, right):
    return jnp.dot(left.astype(jnp.float32), right.astype(jnp.float32), precision=lax.Precision.HIGHEST, preferred_element_type=jnp.float32)

def interest_of(queries, history_rows, length, w_query, w_key, w_pair, a_out):
    n_items = queries.shape[0]
    block_size = math.gcd(n_items, 32)
    k_part = matmul(history_rows, w_key).T
    live_mask = jnp.arange(history_rows.shape[0], dtype=jnp.int32) < length
    pair_rows = w_pair.T.astype(jnp.float32)
    a_vector = a_out.astype(jnp.float32)

    def one_block(q_block):
        q_part = matmul(q_block, w_query)
        scaled = (q_block.astype(jnp.float32)[:, None, :] * pair_rows[None]).astype(jnp.bfloat16)
        raw_pair = matmul(scaled.reshape(-1, scaled.shape[2]), history_rows.T)
        raw_pair = raw_pair.reshape(q_block.shape[0], pair_rows.shape[0], history_rows.shape[0])
        unit_act = jax.nn.relu(raw_pair + q_part[:, :, None] + k_part[None])
        scores = jnp.einsum('bak,a->bk', unit_act, a_vector, precision=lax.Precision.HIGHEST)
        scores = jnp.where(live_mask[None], scores, 0.0).astype(jnp.bfloat16)
        return matmul(scores, history_rows)
    weighted = lax.map(one_block, queries.reshape(n_items // block_size, block_size, queries.shape[1]))
    inv_root = 1.0 / jnp.sqrt(length.astype(jnp.float32))
    return (weighted.reshape(n_items, -1) * inv_root).astype(jnp.bfloat16)

def leaf_embed(leaf_rows, leaf_table):
    tree_count, leaf_count, feat_width = leaf_table.shape
    one_hot = (leaf_rows[..., None] == jnp.arange(leaf_count, dtype=jnp.int32)).astype(jnp.float32)
    one_hot = one_hot.reshape(leaf_rows.shape[0], tree_count * leaf_count)
    return matmul(one_hot, leaf_table.reshape(tree_count * leaf_count, feat_width)).astype(jnp.bfloat16)

def reference(history, lengths, target, bag_ids, leaf_ids, table_piece, leaf_table, w_query, w_key, w_pair, a_out, w_first, w_second, w_third, w_out):
    table_base = jnp.arange(TABLES, dtype=jnp.int32)[None, :, None] * SPLIT

    def one_request(inputs):
        history_rows, length, queries, bag_rows, leaf_rows = inputs
        interest = interest_of(queries, history_rows, length, w_query, w_key, w_pair, a_out)
        piece_ids = bag_rows // PIECE_ROWS
        looked = table_piece[table_base + piece_ids, bag_rows % PIECE_ROWS].astype(jnp.float32)
        pooled = jnp.zeros((looked.shape[0], looked.shape[1], looked.shape[3]), jnp.float32)
        for piece_idx in range(SPLIT):
            part_sum = lax.optimization_barrier(jnp.sum(jnp.where((piece_ids == piece_idx)[..., None], looked, 0.0), axis=2)).astype(jnp.bfloat16)
            pooled = pooled + lax.optimization_barrier(part_sum).astype(jnp.float32)
        pooled = pooled.astype(jnp.bfloat16).reshape(queries.shape[0], -1)
        leaf_vec = leaf_embed(leaf_rows, leaf_table)
        features = jnp.concatenate([pooled, interest, queries, leaf_vec], axis=1)
        hidden_one = jax.nn.relu(matmul(features, w_first)).astype(jnp.bfloat16)
        hidden_two = jax.nn.relu(matmul(hidden_one, w_second)).astype(jnp.bfloat16)
        hidden_three = jax.nn.relu(matmul(hidden_two, w_third)).astype(jnp.bfloat16)
        return matmul(hidden_three, w_out)
    return lax.map(one_request, (history, lengths, target, bag_ids, leaf_ids))
```

```python
import functools

import jax
import jax.numpy as jnp
from jax import lax
from jax.experimental import pallas as pl
from jax.experimental.pallas import tpu as pltpu
from jax.sharding import PartitionSpec as P

MESH = pl.DeviceIdType.MESH
SPLIT = 4
F32 = jnp.float32
BF16 = jnp.bfloat16


class Place:
    def __init__(self, n_grp, n_cand):
        self.n_cand = n_cand
        self.chips_x = n_cand // 2
        self.chips = n_grp * self.chips_x
        self.grp = lax.axis_index("grp")
        self.cand = lax.axis_index("cand")
        self.core = lax.rem(self.cand, 2)
        self.x = lax.div(self.cand, 2)
        self.chip = self.grp * self.chips_x + self.x

    def same_core(self, chip):
        return (lax.div(chip, self.chips_x), 2 * lax.rem(chip, self.chips_x) + self.core)

    def other_core(self, step):
        return (self.grp, 2 * lax.rem(self.x + step, self.chips_x) + 1 - self.core)

    def chip_after(self, step):
        return lax.rem(self.chip + step, self.chips)

    def enter(self):
        barrier = pltpu.get_barrier_semaphore()

        def greet_same(step, carry):
            pl.semaphore_signal(
                barrier, inc=1, device_id=self.same_core(self.chip_after(step)), device_id_type=MESH
            )
            return carry

        lax.fori_loop(1, self.chips, greet_same, 0)
        for step in range(self.chips_x):
            pl.semaphore_signal(barrier, inc=1, device_id=self.other_core(step), device_id_type=MESH)
        return barrier, self.chips - 1 + self.chips_x


def exchange_kernel(
    n_grp, n_cand, ids_ref, target_ref, piece_ref, ids_out, target_out, piece_out,
    ids_send, ids_recv, t_send, t_recv, swap_send, swap_recv, own_sem,
):
    at = Place(n_grp, n_cand)
    barrier, count = at.enter()
    own_ids = pltpu.make_async_copy(ids_ref.at[at.chip], ids_out.at[at.chip], own_sem.at[0])
    own_target = pltpu.make_async_copy(target_ref.at[at.cand], target_out.at[at.cand], own_sem.at[1])
    own_ids.start()
    own_target.start()
    pl.semaphore_wait(barrier, count)

    def send_ids(step):
        to = at.chip_after(step)
        return pltpu.make_async_remote_copy(
            src_ref=ids_ref.at[to], dst_ref=ids_out.at[at.chip],
            send_sem=ids_send.at[step], recv_sem=ids_recv.at[at.chip],
            device_id=at.same_core(to), device_id_type=MESH,
        )

    def from_chip(step):
        chip = at.chip_after(step)
        return pltpu.make_async_remote_copy(
            src_ref=ids_ref.at[chip], dst_ref=ids_out.at[chip],
            send_sem=ids_send.at[step], recv_sem=ids_recv.at[chip],
            device_id=at.same_core(chip), device_id_type=MESH,
        )

    def send_target(step):
        to = lax.rem(at.cand + step, n_cand)
        return pltpu.make_async_remote_copy(
            src_ref=target_ref.at[to], dst_ref=target_out.at[at.cand],
            send_sem=t_send.at[step], recv_sem=t_recv.at[at.cand],
            device_id=(at.grp, to), device_id_type=MESH,
        )

    def target_from(step):
        cand = lax.rem(at.cand + step, n_cand)
        return pltpu.make_async_remote_copy(
            src_ref=target_ref.at[cand], dst_ref=target_out.at[cand],
            send_sem=t_send.at[step], recv_sem=t_recv.at[cand],
            device_id=(at.grp, cand), device_id_type=MESH,
        )

    def loop(first, last, act):
        def body(step, carry):
            act(step)
            return carry

        lax.fori_loop(first, last, body, 0)

    swap = pltpu.make_async_remote_copy(
        src_ref=piece_ref.at[0], dst_ref=piece_out, send_sem=swap_send, recv_sem=swap_recv,
        device_id=at.other_core(0), device_id_type=MESH,
    )
    loop(1, at.chips, lambda step: send_ids(step).start())
    loop(1, n_cand, lambda step: send_target(step).start())
    swap.start()
    own_ids.wait()
    own_target.wait()
    loop(1, n_cand, lambda step: target_from(step).wait_recv())
    loop(1, at.chips, lambda step: from_chip(step).wait_recv())
    loop(1, n_cand, lambda step: send_target(step).wait_send())
    loop(1, at.chips, lambda step: send_ids(step).wait_send())
    swap.wait()


def pool_kernel(bag, per_src, ids_ref, own_ref, other_ref, out_ref, table, total):
    piece_rows = other_ref.shape[0]
    core = lax.rem(lax.axis_index("cand"), 2)
    half = 512

    def widen(i, carry):
        at = pl.multiple_of(i * half, half)
        mine = pl.multiple_of(core * piece_rows + i * half, half)
        theirs = pl.multiple_of((1 - core) * piece_rows + i * half, half)
        table[pl.ds(mine, half), :] = own_ref[0, pl.ds(at, half), :].astype(F32)
        table[pl.ds(theirs, half), :] = other_ref[pl.ds(at, half), :].astype(F32)
        return carry

    lax.fori_loop(0, piece_rows // half, widen, 0)
    table[pl.ds(2 * piece_rows, 8), :] = jnp.zeros((8, table.shape[1]), F32)

    def one_source(src, carry):
        for row in range(per_src):
            total_row = None
            for slot in range(bag):
                at = ids_ref[src, row * bag + slot]
                got = table[pl.ds(at, 1), :]
                total_row = got if total_row is None else total_row + got
            total[pl.ds(src * per_src + row, 1), :] = total_row
        return carry

    lax.fori_loop(0, ids_ref.shape[0], one_source, 0)

    def narrow(src, carry):
        at = pl.multiple_of(src * per_src, per_src)
        out_ref[src] = total[pl.ds(at, per_src), :].astype(BF16)
        return carry

    lax.fori_loop(0, out_ref.shape[0], narrow, 0)


def score_kernel(
    n_grp, n_cand, sums_ref, length_ref, cands_ref, target_ref, leaf_ids_ref, history_hbm,
    leaf_hbm, w_query_ref, w_key_ref, w_pair_ref, a_out_ref, w_first_hbm, w_second_hbm, w_third_hbm,
    w_out_ref, out_ref,
    got, back, interest, history, leaf_table, w_first, w_second, w_third, scores, comb, pooled,
    sum_send, sum_recv, back_send, back_recv, load_sem,
):
    at = Place(n_grp, n_cand)
    barrier, count = at.enter()
    loads = [
        pltpu.make_async_copy(src, dst, load_sem.at[i])
        for i, (src, dst) in enumerate(
            [
                (history_hbm.at[0], history),
                (leaf_hbm, leaf_table),
                (w_first_hbm, w_first),
                (w_second_hbm, w_second),
                (w_third_hbm, w_third),
                (sums_ref.at[at.chip], got.at[at.chip]),
            ]
        )
    ]
    for load in loads:
        load.start()

    def loop(first, last, act):
        def body(step, carry):
            act(step)
            return carry

        lax.fori_loop(first, last, body, 0)

    def send_sums(step):
        to = at.chip_after(step)
        return pltpu.make_async_remote_copy(
            src_ref=sums_ref.at[to], dst_ref=got.at[at.chip],
            send_sem=sum_send.at[step], recv_sem=sum_recv.at[at.chip],
            device_id=at.same_core(to), device_id_type=MESH,
        )

    def sums_from(step):
        chip = at.chip_after(step)
        return pltpu.make_async_remote_copy(
            src_ref=sums_ref.at[chip], dst_ref=got.at[chip],
            send_sem=sum_send.at[step], recv_sem=sum_recv.at[chip],
            device_id=at.same_core(chip), device_id_type=MESH,
        )

    def send_back(step):
        to = lax.rem(at.cand + step, n_cand)
        return pltpu.make_async_remote_copy(
            src_ref=interest.at[to], dst_ref=back.at[at.cand],
            send_sem=back_send.at[step], recv_sem=back_recv.at[at.cand],
            device_id=(at.grp, to), device_id_type=MESH,
        )

    def back_from(step):
        cand = lax.rem(at.cand + step, n_cand)
        return pltpu.make_async_remote_copy(
            src_ref=interest.at[cand], dst_ref=back.at[cand],
            send_sem=back_send.at[step], recv_sem=back_recv.at[cand],
            device_id=(at.grp, cand), device_id_type=MESH,
        )

    pl.semaphore_wait(barrier, count)
    loop(1, at.chips, lambda step: send_sums(step).start())

    loads[0].wait()
    events, width = history.shape
    att = w_pair_ref.shape[1]
    per_src = cands_ref.shape[1]
    pair_t = w_pair_ref[...].astype(F32).T
    key_t = w_key_ref[...].astype(F32).T
    query_t = w_query_ref[...].astype(F32).T.astype(BF16)
    a_col = a_out_ref[...].astype(F32).T
    a_wide = jnp.broadcast_to(a_col, (att, 256))
    history_t = history[...].astype(F32).T.astype(BF16)
    length = length_ref[0]
    column = lax.broadcasted_iota(jnp.int32, (per_src, events), 1)

    def one_group(g, carry):
        rows = cands_ref[g]
        rows_f = rows.astype(F32)
        q_part = lax.dot_general(query_t, rows, (((1,), (1,)), ((), ())), preferred_element_type=F32)
        base = jnp.sum(q_part * a_col, axis=0, keepdims=True)
        for c in range(per_src):
            comb[pl.ds(c * att, att), :] = (rows_f[c : c + 1, :] * pair_t + key_t).astype(BF16)
        for block in range(events // 256):
            cols = pl.ds(block * 256, 256)
            raw = jnp.dot(comb[...], history_t[:, block * 256 : block * 256 + 256], preferred_element_type=F32)
            for c in range(per_src):
                unit = jnp.maximum(raw[c * att : (c + 1) * att, :], -q_part[:, c : c + 1]) * a_wide
                line = jnp.sum(unit, axis=0, keepdims=True) + base[:, c : c + 1]
                scores[pl.ds(g * per_src + c, 1), cols] = line
        return carry

    lax.fori_loop(0, n_cand, one_group, 0)
    live = lax.broadcasted_iota(jnp.int32, scores.shape, 1) < length
    weights = jnp.where(live, scores[...], 0.0).astype(BF16)
    weighted = jnp.dot(weights, history[...], preferred_element_type=F32)
    root = jnp.sqrt(jnp.full((1, 1), length, jnp.int32).astype(F32))
    weighted = weighted * (1.0 / root)
    interest[...] = weighted.reshape(interest.shape)

    loads[1].wait()
    n_rows, trees = leaf_ids_ref.shape
    leaves = leaf_table.shape[0] // trees
    spread_row = lax.broadcasted_iota(jnp.int32, (trees, trees * leaves), 0)
    spread_col = lax.broadcasted_iota(jnp.int32, (trees, trees * leaves), 1)
    spread = (spread_row == spread_col // leaves).astype(F32).astype(BF16)
    ids = leaf_ids_ref[...].astype(F32).astype(BF16)
    wide = jnp.dot(ids, spread, preferred_element_type=F32)
    leaf_of = lax.broadcasted_iota(jnp.int32, wide.shape, 1) % leaves
    hot = (wide == leaf_of.astype(F32)).astype(F32).astype(BF16)
    leaf_vec = jnp.dot(hot, leaf_table[...], preferred_element_type=F32).astype(BF16)

    loop(1, n_cand, lambda step: send_back(step).start())
    back[at.cand] = interest[at.cand]

    loads[2].wait()
    table_width = w_first.shape[0] - 3 * width
    hidden = jnp.dot(
        target_ref[...], w_first[pl.ds(table_width + width, width), :], preferred_element_type=F32
    )
    hidden += jnp.dot(leaf_vec, w_first[pl.ds(table_width + 2 * width, width), :], preferred_element_type=F32)

    loads[3].wait()
    loads[4].wait()
    loads[5].wait()
    loop(1, n_cand, lambda step: back_from(step).wait_recv())
    seen = back[...].reshape(n_rows, width).astype(BF16)
    hidden += jnp.dot(seen, w_first[pl.ds(table_width, width), :], preferred_element_type=F32)
    loop(1, at.chips, lambda step: sums_from(step).wait_recv())
    emb = got.shape[2]
    for t in range(got.shape[0] // 2):
        pooled[:, pl.ds(t * emb, emb)] = (got[2 * t].astype(F32) + got[2 * t + 1].astype(F32)).astype(BF16)
    hidden += jnp.dot(pooled[...], w_first[pl.ds(0, table_width), :], preferred_element_type=F32)

    one = jnp.maximum(hidden, 0.0).astype(BF16)
    two = jnp.maximum(jnp.dot(one, w_second[...], preferred_element_type=F32), 0.0).astype(BF16)
    three = jnp.maximum(jnp.dot(two, w_third[...], preferred_element_type=F32), 0.0).astype(BF16)
    logit = jnp.sum(three.astype(F32) * w_out_ref[...].astype(F32), axis=1, keepdims=True)
    n_req, per_req = out_ref.shape
    row = lax.broadcasted_iota(jnp.int32, (n_rows, 128), 0) % per_req
    lane = lax.broadcasted_iota(jnp.int32, (n_rows, 128), 1)
    placed = jnp.where(row == lane, logit, 0.0).reshape(n_req, per_req, 128)
    out_ref[...] = jnp.sum(placed, axis=1)[:, :per_req]

    loop(1, n_cand, lambda step: send_back(step).wait_send())
    loop(1, at.chips, lambda step: send_sums(step).wait_send())


def on_device(
    n_grp, n_cand, history, lengths, target, bag_ids, leaf_ids, table_piece, leaf_table,
    w_query, w_key, w_pair, a_out, w_first, w_second, w_third, w_out,
):
    n_req, per_req, width = target.shape
    rows = n_req * per_req
    _, _, tables, bag = bag_ids.shape
    _, piece_rows, emb = table_piece.shape
    _, events, _ = history.shape
    trees, leaves, _ = leaf_table.shape
    att = w_pair.shape[1]
    chips = n_grp * n_cand // 2
    halves = chips // tables
    half_rows = 2 * piece_rows
    dma = pltpu.SemaphoreType.DMA
    hbm = pl.BlockSpec(memory_space=pl.ANY)
    vmem = pl.BlockSpec(memory_space=pltpu.VMEM)
    smem = pl.BlockSpec(memory_space=pltpu.SMEM)

    by_table = jnp.transpose(bag_ids.reshape(rows, tables, bag), (1, 0, 2)).reshape(tables, 1, rows * bag)
    half_of = jnp.arange(halves, dtype=jnp.int32).reshape(1, halves, 1)
    local = by_table - half_of * half_rows
    inside = (local >= 0) & (local < half_rows)
    ids = jnp.where(inside, local, half_rows).reshape(chips, 1, rows * bag)

    got_ids, cands, other_piece = pl.pallas_call(
        functools.partial(exchange_kernel, n_grp, n_cand),
        out_shape=(
            jax.ShapeDtypeStruct(ids.shape, jnp.int32),
            jax.ShapeDtypeStruct((n_cand, per_req, width), BF16),
            jax.ShapeDtypeStruct((piece_rows, emb), BF16),
        ),
        in_specs=[hbm] * 3,
        out_specs=(hbm,) * 3,
        scratch_shapes=[
            dma((chips,)), dma((chips,)), dma((n_cand,)), dma((n_cand,)), dma(()), dma(()), dma((2,)),
        ],
        compiler_params=pltpu.CompilerParams(collective_id=0, has_side_effects=True),
        name="exchange",
    )(ids, target, table_piece)

    sums = pl.pallas_call(
        functools.partial(pool_kernel, bag, rows),
        out_shape=jax.ShapeDtypeStruct((chips, rows, emb), BF16),
        in_specs=[smem, vmem, vmem],
        out_specs=vmem,
        scratch_shapes=[
            pltpu.VMEM((half_rows + 8, emb), F32),
            pltpu.VMEM((chips * rows, emb), F32),
        ],
        name="pool",
    )(got_ids.reshape(chips, rows * bag), table_piece, other_piece)

    return pl.pallas_call(
        functools.partial(score_kernel, n_grp, n_cand),
        out_shape=jax.ShapeDtypeStruct((n_req, per_req), F32),
        in_specs=[hbm, smem, vmem, vmem, vmem, hbm, hbm, vmem, vmem, vmem, vmem, hbm, hbm, hbm, vmem],
        out_specs=vmem,
        scratch_shapes=[
            pltpu.VMEM((chips, rows, emb), BF16),
            pltpu.VMEM((n_cand, per_req, width), F32),
            pltpu.VMEM((n_cand, per_req, width), F32),
            pltpu.VMEM((events, width), BF16),
            pltpu.VMEM((trees * leaves, width), BF16),
            pltpu.VMEM(w_first.shape, BF16),
            pltpu.VMEM(w_second.shape, BF16),
            pltpu.VMEM(w_third.shape, BF16),
            pltpu.VMEM((rows, events), F32),
            pltpu.VMEM((per_req * att, width), BF16),
            pltpu.VMEM((rows, tables * emb), BF16),
            dma((chips,)), dma((chips,)), dma((n_cand,)), dma((n_cand,)), dma((6,)),
        ],
        compiler_params=pltpu.CompilerParams(
            collective_id=1, has_side_effects=True, vmem_limit_bytes=56 * 1024 * 1024
        ),
        name="score",
    )(
        sums, lengths, cands, target.reshape(rows, width), leaf_ids.reshape(rows, trees), history,
        leaf_table.reshape(trees * leaves, width), w_query, w_key, w_pair, a_out.reshape(1, att),
        w_first, w_second, w_third, w_out.reshape(1, -1),
    )


def solution(mesh):
    n_grp, n_cand = mesh.shape["grp"], mesh.shape["cand"]
    both = ("grp", "cand")
    placed = (
        P(both, None, None), P(both), P("grp", "cand", None), P("grp", "cand", None, None),
        P("grp", "cand", None), P(both, None, None),
    ) + (P(),) * 9
    return jax.shard_map(
        functools.partial(on_device, n_grp, n_cand),
        mesh=mesh, in_specs=placed, out_specs=P("grp", "cand"), check_vma=False,
    )
```

```python
import functools

import jax
import jax.numpy as jnp
from jax import lax
from jax.experimental import pallas as pl
from jax.experimental.pallas import tpu as pltpu
from jax.sharding import PartitionSpec as P

MESH = pl.DeviceIdType.MESH
PARTS = 4
STRIDE = 27
F32 = jnp.float32
BF16 = jnp.bfloat16


class Place:
    def __init__(self, n_grp, n_cand):
        self.n_cand = n_cand
        self.chips_x = n_cand // 2
        self.chips = n_grp * self.chips_x
        self.grp = lax.axis_index("grp")
        self.cand = lax.axis_index("cand")
        self.core = lax.rem(self.cand, 2)
        self.x = lax.div(self.cand, 2)
        self.chip = self.grp * self.chips_x + self.x

    def same_core(self, chip):
        return (lax.div(chip, self.chips_x), 2 * lax.rem(chip, self.chips_x) + self.core)

    def other_core(self, step):
        return (self.grp, 2 * lax.rem(self.x + step, self.chips_x) + 1 - self.core)

    def chip_after(self, step):
        return lax.rem(self.chip + step, self.chips)

    def enter(self):
        barrier = pltpu.get_barrier_semaphore()

        def greet_same(step, carry):
            pl.semaphore_signal(
                barrier, inc=1, device_id=self.same_core(self.chip_after(step)), device_id_type=MESH
            )
            return carry

        lax.fori_loop(1, self.chips, greet_same, 0)
        for step in range(self.chips_x):
            pl.semaphore_signal(barrier, inc=1, device_id=self.other_core(step), device_id_type=MESH)
        return barrier, self.chips - 1 + self.chips_x


def repeat(first, last, act):
    def body(step, carry):
        act(step)
        return carry

    lax.fori_loop(first, last, body, 0)


def kernel(
    n_grp, n_cand, bag_hbm, length_hbm, target_hbm, rows_hbm, leaf_ids_hbm, history_hbm, leaf_hbm, piece_hbm,
    w_query_hbm, w_key_hbm, w_pair_hbm, a_out_hbm, w_first_hbm, w_second_hbm, w_third_hbm, w_out_hbm,
    out_ref,
    bags, length_s, target, target_rows, leaf_ids, history, leaf_table, own, w_query, w_key, w_pair, a_out,
    w_first, w_second, w_third, w_out,
    ids_stage, ids_got, ids_s, other, table, total, sums, got, cands, back, interest, scores, comb, pooled, hidden_ref,
    load_sem, ids_send, ids_recv, ids_sem, swap_send, swap_recv, t_send, t_recv,
    sum_send, sum_recv, back_send, back_recv,
):
    at = Place(n_grp, n_cand)
    barrier, count = at.enter()
    pairs = dict(
        bags=(bag_hbm, bags), own=(piece_hbm.at[0], own), target=(target_hbm, target),
        w_pair=(w_pair_hbm, w_pair), w_key=(w_key_hbm, w_key), w_query=(w_query_hbm, w_query),
        a_out=(a_out_hbm, a_out), history=(history_hbm.at[0], history), leaf_ids=(leaf_ids_hbm, leaf_ids),
        leaf=(leaf_hbm, leaf_table), rows=(rows_hbm, target_rows), length=(length_hbm, length_s),
        w_first=(w_first_hbm, w_first), w_second=(w_second_hbm, w_second), w_third=(w_third_hbm, w_third),
        w_out=(w_out_hbm, w_out),
    )
    loads = {
        name: pltpu.make_async_copy(src, dst, load_sem.at[i])
        for i, (name, (src, dst)) in enumerate(pairs.items())
    }
    for load in loads.values():
        load.start()

    n_rows, bag, tables = bags.shape
    piece_rows, emb = other.shape
    half_rows = 2 * piece_rows
    halves = at.chips // tables
    parts = PARTS
    part = piece_rows // parts

    loads["bags"].wait()
    turned = [bags[:, slot, :].T for slot in range(bag)]
    for half in range(halves):
        for slot in range(0, bag, 2):
            both = jnp.concatenate(turned[slot : slot + 2], axis=1) - half * half_rows
            both = jnp.where((both >= 0) & (both < half_rows), both, half_rows)
            ids_stage[half, :, 0, pl.ds(slot * n_rows, 2 * n_rows)] = both

    def send_ids(step):
        to = at.chip_after(step)
        return pltpu.make_async_remote_copy(
            src_ref=ids_stage.at[lax.rem(to, halves), lax.div(to, halves)], dst_ref=ids_got.at[at.chip],
            send_sem=ids_send.at[step], recv_sem=ids_recv.at[at.chip],
            device_id=at.same_core(to), device_id_type=MESH,
        )

    def ids_from(step):
        chip = at.chip_after(step)
        return pltpu.make_async_remote_copy(
            src_ref=ids_stage.at[0, 0], dst_ref=ids_got.at[chip],
            send_sem=ids_send.at[step], recv_sem=ids_recv.at[chip],
            device_id=at.same_core(chip), device_id_type=MESH,
        )

    def send_target(step):
        to = lax.rem(at.cand + step, n_cand)
        return pltpu.make_async_remote_copy(
            src_ref=target.at[to], dst_ref=cands.at[at.cand],
            send_sem=t_send.at[step], recv_sem=t_recv.at[at.cand],
            device_id=(at.grp, to), device_id_type=MESH,
        )

    def target_from(step):
        cand = lax.rem(at.cand + step, n_cand)
        return pltpu.make_async_remote_copy(
            src_ref=target.at[cand], dst_ref=cands.at[cand],
            send_sem=t_send.at[step], recv_sem=t_recv.at[cand],
            device_id=(at.grp, cand), device_id_type=MESH,
        )

    def swap(i):
        rows = pl.ds(i * part, part)
        return pltpu.make_async_remote_copy(
            src_ref=own.at[rows], dst_ref=other.at[rows],
            send_sem=swap_send.at[i], recv_sem=swap_recv.at[i],
            device_id=at.other_core(0), device_id_type=MESH,
        )

    def source(step):
        return at.chip_after(lax.rem(step * STRIDE, at.chips))

    def send_sums(step):
        to = source(step)
        return pltpu.make_async_remote_copy(
            src_ref=sums.at[to], dst_ref=got.at[at.chip],
            send_sem=sum_send.at[step], recv_sem=sum_recv.at[at.chip],
            device_id=at.same_core(to), device_id_type=MESH,
        )

    def sums_from(step):
        chip = at.chip_after(step)
        return pltpu.make_async_remote_copy(
            src_ref=sums.at[chip], dst_ref=got.at[chip],
            send_sem=sum_send.at[step], recv_sem=sum_recv.at[chip],
            device_id=at.same_core(chip), device_id_type=MESH,
        )

    def send_back(step):
        to = lax.rem(at.cand + step, n_cand)
        return pltpu.make_async_remote_copy(
            src_ref=interest.at[to], dst_ref=back.at[at.cand],
            send_sem=back_send.at[step], recv_sem=back_recv.at[at.cand],
            device_id=(at.grp, to), device_id_type=MESH,
        )

    def back_from(step):
        cand = lax.rem(at.cand + step, n_cand)
        return pltpu.make_async_remote_copy(
            src_ref=interest.at[cand], dst_ref=back.at[cand],
            send_sem=back_send.at[step], recv_sem=back_recv.at[cand],
            device_id=(at.grp, cand), device_id_type=MESH,
        )

    chunk = 512

    def widen(piece, core, first, rows):
        def step(i):
            here = pl.multiple_of(first + i * chunk, chunk)
            there = pl.multiple_of(core * piece_rows + first + i * chunk, chunk)
            table[pl.ds(there, chunk), :] = piece[pl.ds(here, chunk), :].astype(F32)

        repeat(0, rows // chunk, step)

    loads["own"].wait()
    widen(own, at.core, 0, piece_rows)
    table[pl.ds(half_rows, 8), :] = jnp.zeros((8, emb), F32)
    total[...] = jnp.zeros_like(total)
    loads["target"].wait()
    cands[at.cand] = target[at.cand]
    ids_got[at.chip] = ids_stage[lax.rem(at.chip, halves), lax.div(at.chip, halves)]
    for name in ("w_pair", "w_key", "w_query", "a_out", "history"):
        loads[name].wait()
    events, width = history.shape
    att = w_pair.shape[1]
    per_src = cands.shape[1]
    pair_t = w_pair[...].astype(F32).T
    key_t = w_key[...].astype(F32).T
    query_t = w_query[...].astype(F32).T.astype(BF16)
    a_col = a_out[...].astype(F32).T
    a_wide = jnp.broadcast_to(a_col, (att, 256))
    history_t = history[...].astype(F32).T.astype(BF16)

    pl.semaphore_wait(barrier, count)
    repeat(1, at.chips, lambda step: send_ids(step).start())
    repeat(1, n_cand, lambda step: send_target(step).start())
    for i in range(parts):
        swap(i).start()

    for name in ("leaf_ids", "leaf", "rows", "length", "w_first"):
        loads[name].wait()
    trees = leaf_ids.shape[1]
    leaves = leaf_table.shape[0] // trees
    spread_row = lax.broadcasted_iota(jnp.int32, (trees, trees * leaves), 0)
    spread_col = lax.broadcasted_iota(jnp.int32, (trees, trees * leaves), 1)
    spread = (spread_row == spread_col // leaves).astype(F32).astype(BF16)
    wide = jnp.dot(leaf_ids[...].astype(F32).astype(BF16), spread, preferred_element_type=F32)
    leaf_of = lax.broadcasted_iota(jnp.int32, wide.shape, 1) % leaves
    hot = (wide == leaf_of.astype(F32)).astype(F32).astype(BF16)
    leaf_vec = jnp.dot(hot, leaf_table[...], preferred_element_type=F32).astype(BF16)
    table_width = w_first.shape[0] - 3 * width
    hidden_ref[...] = jnp.dot(
        target_rows[...], w_first[pl.ds(table_width + width, width), :], preferred_element_type=F32
    ) + jnp.dot(leaf_vec, w_first[pl.ds(table_width + 2 * width, width), :], preferred_element_type=F32)

    repeat(1, n_cand, lambda step: target_from(step).wait_recv())
    length = length_s[0]

    def one_group(g):
        rows_f = cands[g].astype(F32)
        q_part = lax.dot_general(query_t, cands[g], (((1,), (1,)), ((), ())), preferred_element_type=F32)
        base = jnp.sum(q_part * a_col, axis=0, keepdims=True)
        for c in range(per_src):
            comb[pl.ds(c * att, att), :] = (rows_f[c : c + 1, :] * pair_t + key_t).astype(BF16)
        for block in range(events // 256):
            cols = pl.ds(block * 256, 256)
            raw = jnp.dot(comb[...], history_t[:, block * 256 : block * 256 + 256], preferred_element_type=F32)
            for c in range(per_src):
                unit = jnp.maximum(raw[c * att : (c + 1) * att, :], -q_part[:, c : c + 1]) * a_wide
                line = jnp.sum(unit, axis=0, keepdims=True) + base[:, c : c + 1]
                scores[pl.ds(g * per_src + c, 1), cols] = line

    repeat(0, n_cand, one_group)
    live = lax.broadcasted_iota(jnp.int32, scores.shape, 1) < length
    weights = jnp.where(live, scores[...], 0.0).astype(BF16)
    weighted = jnp.dot(weights, history[...], preferred_element_type=F32)
    root = jnp.sqrt(jnp.full((1, 1), length, jnp.int32).astype(F32))
    weighted = weighted * (1.0 / root)
    interest[...] = weighted.reshape(interest.shape)

    repeat(1, at.chips, lambda step: ids_from(step).wait_recv())
    to_scalar = pltpu.make_async_copy(ids_got, ids_s, ids_sem)
    to_scalar.start()
    for i in range(parts):
        swap(i).wait_recv()
        widen(other, 1 - at.core, i * part, part)
    back[at.cand] = interest[at.cand]
    repeat(1, n_cand, lambda step: send_back(step).start())
    to_scalar.wait()

    def one_source(step):
        src = source(step)

        @pl.when(step >= 3)
        def _():
            send_sums(step - 2).start()

        sums[source(step + at.chips - 1)] = total[...].astype(BF16)
        for row in range(n_rows):
            row_sum = None
            for slot in range(bag):
                line = table[pl.ds(ids_s[src, 0, slot * n_rows + row], 1), :]
                row_sum = line if row_sum is None else row_sum + line
            total[pl.ds(row, 1), :] = row_sum

    repeat(0, at.chips, one_source)
    sums[source(at.chips - 1)] = total[...].astype(BF16)
    send_sums(at.chips - 2).start()
    got[at.chip] = sums[at.chip]
    repeat(1, n_cand, lambda step: back_from(step).wait_recv())
    seen = back[...].reshape(n_rows, width).astype(BF16)
    hidden = hidden_ref[...] + jnp.dot(seen, w_first[pl.ds(table_width, width), :], preferred_element_type=F32)
    send_sums(at.chips - 1).start()
    for name in ("w_second", "w_third", "w_out"):
        loads[name].wait()
    repeat(1, at.chips, lambda step: sums_from(step).wait_recv())
    for t in range(tables):
        pooled[:, pl.ds(t * emb, emb)] = (got[2 * t].astype(F32) + got[2 * t + 1].astype(F32)).astype(BF16)
    hidden += jnp.dot(pooled[...], w_first[pl.ds(0, table_width), :], preferred_element_type=F32)
    one = jnp.maximum(hidden, 0.0).astype(BF16)
    two = jnp.maximum(jnp.dot(one, w_second[...], preferred_element_type=F32), 0.0).astype(BF16)
    three = jnp.maximum(jnp.dot(two, w_third[...], preferred_element_type=F32), 0.0).astype(BF16)
    logit = jnp.sum(three.astype(F32) * w_out[...].astype(F32), axis=1, keepdims=True)
    n_req, per_req = out_ref.shape
    row = lax.broadcasted_iota(jnp.int32, (n_rows, 128), 0) % per_req
    lane = lax.broadcasted_iota(jnp.int32, (n_rows, 128), 1)
    placed = jnp.where(row == lane, logit, 0.0).reshape(n_req, per_req, 128)
    out_ref[...] = jnp.sum(placed, axis=1)[:, :per_req]

    repeat(1, at.chips, lambda step: send_ids(step).wait_send())
    repeat(1, n_cand, lambda step: send_target(step).wait_send())
    for i in range(parts):
        swap(i).wait_send()
    repeat(1, n_cand, lambda step: send_back(step).wait_send())
    repeat(1, at.chips, lambda step: send_sums(step).wait_send())


def on_device(
    n_grp, n_cand, history, lengths, target, bag_ids, leaf_ids, table_piece, leaf_table,
    w_query, w_key, w_pair, a_out, w_first, w_second, w_third, w_out,
):
    n_req, per_req, width = target.shape
    rows = n_req * per_req
    _, _, tables, bag = bag_ids.shape
    _, piece_rows, emb = table_piece.shape
    _, events, _ = history.shape
    trees, leaves, _ = leaf_table.shape
    att = w_pair.shape[1]
    chips = n_grp * n_cand // 2
    halves = chips // tables
    dma = pltpu.SemaphoreType.DMA
    hbm = pl.BlockSpec(memory_space=pl.ANY)

    args = (
        jnp.transpose(bag_ids, (0, 1, 3, 2)).reshape(rows, bag, tables), lengths, target,
        target.reshape(rows, width), leaf_ids.reshape(rows, trees), history,
        leaf_table.reshape(trees * leaves, width), table_piece, w_query, w_key, w_pair, a_out.reshape(1, att),
        w_first, w_second, w_third, w_out.reshape(1, -1),
    )

    def held(i):
        return pltpu.VMEM(args[i].shape, args[i].dtype)

    return pl.pallas_call(
        functools.partial(kernel, n_grp, n_cand),
        out_shape=jax.ShapeDtypeStruct((n_req, per_req), F32),
        in_specs=[hbm] * len(args),
        out_specs=pl.BlockSpec(memory_space=pltpu.VMEM),
        scratch_shapes=[
            held(0), pltpu.SMEM((1,), jnp.int32), held(2), held(3), held(4), pltpu.VMEM((events, width), BF16),
            held(6), pltpu.VMEM((piece_rows, emb), BF16), held(8), held(9), held(10), held(11),
            held(12), held(13), held(14), held(15),
            pltpu.VMEM((halves, tables, 1, rows * bag), jnp.int32),
            pltpu.VMEM((chips, 1, rows * bag), jnp.int32),
            pltpu.SMEM((chips, 1, rows * bag), jnp.int32),
            pltpu.VMEM((piece_rows, emb), BF16),
            pltpu.VMEM((2 * piece_rows + 8, emb), F32),
            pltpu.VMEM((rows, emb), F32),
            pltpu.VMEM((chips, rows, emb), BF16),
            pltpu.VMEM((chips, rows, emb), BF16),
            pltpu.VMEM((n_cand, per_req, width), BF16),
            pltpu.VMEM((n_cand, per_req, width), F32),
            pltpu.VMEM((n_cand, per_req, width), F32),
            pltpu.VMEM((rows, events), F32),
            pltpu.VMEM((per_req * att, width), BF16),
            pltpu.VMEM((rows, tables * emb), BF16),
            pltpu.VMEM((rows, w_first.shape[1]), F32),
            dma((len(args),)), dma((chips,)), dma((chips,)), dma(()), dma((PARTS,)), dma((PARTS,)),
            dma((n_cand,)), dma((n_cand,)), dma((chips,)), dma((chips,)), dma((n_cand,)), dma((n_cand,)),
        ],
        compiler_params=pltpu.CompilerParams(
            collective_id=0, has_side_effects=True, vmem_limit_bytes=56 * 1024 * 1024
        ),
        name="rank",
    )(*args)


def solution(mesh):
    n_grp, n_cand = mesh.shape["grp"], mesh.shape["cand"]
    both = ("grp", "cand")
    placed = (
        P(both, None, None), P(both), P("grp", "cand", None), P("grp", "cand", None, None),
        P("grp", "cand", None), P(both, None, None),
    ) + (P(),) * 9
    return jax.shard_map(
        functools.partial(on_device, n_grp, n_cand),
        mesh=mesh, in_specs=placed, out_specs=P("grp", "cand"), check_vma=False,
    )
```

```python
import functools
import math

import jax
import jax.numpy as jnp
from jax import lax
from jax.experimental import pallas as pl
from jax.experimental.pallas import tpu as pltpu
from jax.sharding import PartitionSpec as P

MESH = pl.DeviceIdType.MESH
PARTS = 4
EARLY = 3
F32 = jnp.float32
BF16 = jnp.bfloat16


class Place:
    def __init__(self, n_grp, n_cand):
        self.side = math.isqrt(n_grp)
        self.chips_x = n_cand // 2
        self.chips = n_grp * self.chips_x
        self.grp = lax.axis_index("grp")
        self.cand = lax.axis_index("cand")
        self.core = lax.rem(self.cand, 2)
        self.x = lax.div(self.cand, 2)
        self.z = lax.div(self.grp, self.side)
        self.chip = self.grp * self.chips_x + self.x
        y = lax.rem(self.grp, self.side)
        self.ys = [lax.rem(y + dy, self.side) for dy in range(self.side)]
        self.xs = [lax.rem(self.x + dx, self.chips_x) for dx in range(self.chips_x)]
        far_y = sorted(range(self.side), key=lambda d: -min(d, self.side - d))
        far_x = sorted(range(self.chips_x), key=lambda d: -min(d, self.chips_x - d))
        self.steps = [(dy, dx) for dy in far_y for dx in far_x]

    def plane(self, j):
        dz = 2 - j + 3 * (j // 2) - 2 * (j // 3) if isinstance(j, int) else (
            2 - j + 3 * lax.div(j, 2) - 2 * lax.div(j, 3)
        )
        return lax.rem(self.z + dz, self.side) * self.side

    def plane_from(self, j):
        dz = 2 + j - 3 * lax.div(j, 2) + 2 * lax.div(j, 3)
        return lax.rem(self.z + dz, self.side) * self.side

    def chip_in(self, plane, i):
        dy, dx = self.steps[i]
        return (plane + self.ys[dy]) * self.chips_x + self.xs[dx]

    def same_core(self, plane, i):
        dy, dx = self.steps[i]
        return (plane + self.ys[dy], 2 * self.xs[dx] + self.core)

    def other_core(self, step):
        return (self.grp, 2 * self.xs[step] + 1 - self.core)

    def chip_after(self, step):
        return lax.rem(self.chip + step, self.chips)

    def each_other_chip(self, act):
        def far(j):
            plane = self.plane(j)
            for i in range(len(self.steps)):
                act(plane, i)

        repeat(0, self.side - 1, far)
        for i in range(len(self.steps) - 1):
            act(self.grp - self.ys[0], i)

    def enter(self):
        barrier = pltpu.get_barrier_semaphore()
        self.each_other_chip(
            lambda plane, i: pl.semaphore_signal(
                barrier, inc=1, device_id=self.same_core(plane, i), device_id_type=MESH
            )
        )
        for step in range(self.chips_x):
            pl.semaphore_signal(barrier, inc=1, device_id=self.other_core(step), device_id_type=MESH)
        return barrier, self.chips - 1 + self.chips_x


def repeat(first, last, act):
    def body(step, carry):
        act(step)
        return carry

    lax.fori_loop(first, last, body, 0)


def kernel(
    n_grp, n_cand, bag_hbm, length_hbm, target_hbm, rows_hbm, leaf_ids_hbm, history_hbm, leaf_hbm, piece_hbm,
    w_query_hbm, w_key_hbm, w_pair_hbm, a_out_hbm, w_first_hbm, w_second_hbm, w_third_hbm, w_out_hbm,
    out_ref,
    bags, length_s, target, target_rows, leaf_ids, history, leaf_table, own, w_query, w_key, w_pair, a_out,
    w_first, w_second, w_third, w_out,
    ids_stage, ids_got, ids_s, other, table, total, sums, got, cands, back, interest, scores, comb, pooled, hidden_ref,
    load_sem, ids_send, ids_recv, ids_sem, swap_send, swap_recv, t_send, t_recv,
    sum_send, sum_recv, back_send, back_recv,
):
    at = Place(n_grp, n_cand)
    barrier, count = at.enter()
    pairs = dict(
        bags=(bag_hbm, bags), own=(piece_hbm.at[0], own), target=(target_hbm, target),
        w_pair=(w_pair_hbm, w_pair), w_key=(w_key_hbm, w_key), w_query=(w_query_hbm, w_query),
        a_out=(a_out_hbm, a_out), history=(history_hbm.at[0], history), leaf_ids=(leaf_ids_hbm, leaf_ids),
        leaf=(leaf_hbm, leaf_table), rows=(rows_hbm, target_rows), length=(length_hbm, length_s),
        w_first=(w_first_hbm, w_first), w_second=(w_second_hbm, w_second), w_third=(w_third_hbm, w_third),
        w_out=(w_out_hbm, w_out),
    )
    loads = {
        name: pltpu.make_async_copy(src, dst, load_sem.at[i])
        for i, (name, (src, dst)) in enumerate(pairs.items())
    }
    for load in loads.values():
        load.start()

    n_rows, bag, tables = bags.shape
    piece_rows, emb = other.shape
    half_rows = 2 * piece_rows
    halves = at.chips // tables
    parts = PARTS
    part = piece_rows // parts

    loads["bags"].wait()
    turned = [bags[:, slot, :].T for slot in range(bag)]
    for half in range(halves):
        for slot in range(0, bag, 2):
            both = jnp.concatenate(turned[slot : slot + 2], axis=1) - half * half_rows
            both = jnp.where((both >= 0) & (both < half_rows), both, half_rows)
            ids_stage[:, half, 0, pl.ds(slot * n_rows, 2 * n_rows)] = both

    def staged(chip):
        return ids_stage.at[lax.div(chip, halves), lax.rem(chip, halves)]

    def send_ids(plane, i):
        to = at.chip_in(plane, i)
        return pltpu.make_async_remote_copy(
            src_ref=staged(to), dst_ref=ids_got.at[at.chip],
            send_sem=ids_send.at[to], recv_sem=ids_recv.at[at.chip],
            device_id=at.same_core(plane, i), device_id_type=MESH,
        )

    def ids_of(chip):
        return pltpu.make_async_remote_copy(
            src_ref=ids_stage.at[0, 0], dst_ref=ids_got.at[chip],
            send_sem=ids_send.at[chip], recv_sem=ids_recv.at[chip],
            device_id=at.other_core(0), device_id_type=MESH,
        )

    own_ids = pltpu.make_async_copy(staged(at.chip), ids_got.at[at.chip], ids_recv.at[at.chip])

    def send_target(step):
        to = lax.rem(at.cand + step, n_cand)
        return pltpu.make_async_remote_copy(
            src_ref=target.at[to], dst_ref=cands.at[at.cand],
            send_sem=t_send.at[step], recv_sem=t_recv.at[at.cand],
            device_id=(at.grp, to), device_id_type=MESH,
        )

    def target_from(step):
        cand = lax.rem(at.cand + step, n_cand)
        return pltpu.make_async_remote_copy(
            src_ref=target.at[cand], dst_ref=cands.at[cand],
            send_sem=t_send.at[step], recv_sem=t_recv.at[cand],
            device_id=(at.grp, cand), device_id_type=MESH,
        )

    def swap(i):
        rows = pl.ds(i * part, part)
        return pltpu.make_async_remote_copy(
            src_ref=own.at[rows], dst_ref=other.at[rows],
            send_sem=swap_send.at[i], recv_sem=swap_recv.at[i],
            device_id=at.other_core(0), device_id_type=MESH,
        )

    def send_sums(plane, i):
        to = at.chip_in(plane, i)
        return pltpu.make_async_remote_copy(
            src_ref=sums.at[to], dst_ref=got.at[at.chip],
            send_sem=sum_send.at[to], recv_sem=sum_recv.at[at.chip],
            device_id=at.same_core(plane, i), device_id_type=MESH,
        )

    def sums_of(chip):
        return pltpu.make_async_remote_copy(
            src_ref=sums.at[chip], dst_ref=got.at[chip],
            send_sem=sum_send.at[chip], recv_sem=sum_recv.at[chip],
            device_id=at.other_core(0), device_id_type=MESH,
        )

    def send_back(step):
        to = lax.rem(at.cand + step, n_cand)
        return pltpu.make_async_remote_copy(
            src_ref=interest.at[to], dst_ref=back.at[at.cand],
            send_sem=back_send.at[step], recv_sem=back_recv.at[at.cand],
            device_id=(at.grp, to), device_id_type=MESH,
        )

    def back_from(step):
        cand = lax.rem(at.cand + step, n_cand)
        return pltpu.make_async_remote_copy(
            src_ref=interest.at[cand], dst_ref=back.at[cand],
            send_sem=back_send.at[step], recv_sem=back_recv.at[cand],
            device_id=(at.grp, cand), device_id_type=MESH,
        )

    chunk = 512

    def widen(piece, core, first, rows):
        def step(i):
            here = pl.multiple_of(first + i * chunk, chunk)
            there = pl.multiple_of(core * piece_rows + first + i * chunk, chunk)
            table[pl.ds(there, chunk), :] = piece[pl.ds(here, chunk), :].astype(F32)

        repeat(0, rows // chunk, step)

    loads["own"].wait()
    widen(own, at.core, 0, piece_rows)
    table[pl.ds(half_rows, 8), :] = jnp.zeros((8, emb), F32)
    loads["target"].wait()
    cands[at.cand] = target[at.cand]
    for name in ("w_pair", "w_key", "w_query", "a_out", "history"):
        loads[name].wait()
    events, width = history.shape
    att = w_pair.shape[1]
    per_src = cands.shape[1]
    pair_t = w_pair[...].astype(F32).T
    key_t = w_key[...].astype(F32).T
    query_t = w_query[...].astype(F32).T.astype(BF16)
    a_col = a_out[...].astype(F32).T
    a_wide = jnp.broadcast_to(a_col, (att, 256))
    history_t = history[...].astype(F32).T.astype(BF16)

    def one_group(step):
        g = lax.rem(at.cand + step, n_cand)
        rows_f = cands[g].astype(F32)
        q_part = lax.dot_general(query_t, cands[g], (((1,), (1,)), ((), ())), preferred_element_type=F32)
        base = jnp.sum(q_part * a_col, axis=0, keepdims=True)
        for c in range(per_src):
            comb[pl.ds(c * att, att), :] = (rows_f[c : c + 1, :] * pair_t + key_t).astype(BF16)
        for block in range(events // 256):
            cols = pl.ds(block * 256, 256)
            raw = jnp.dot(comb[...], history_t[:, block * 256 : block * 256 + 256], preferred_element_type=F32)
            for c in range(per_src):
                unit = jnp.maximum(raw[c * att : (c + 1) * att, :], -q_part[:, c : c + 1]) * a_wide
                line = jnp.sum(unit, axis=0, keepdims=True) + base[:, c : c + 1]
                scores[pl.ds(g * per_src + c, 1), cols] = line

    def arrived_group(step):
        target_from(step).wait_recv()
        one_group(step)

    one_group(0)

    pl.semaphore_wait(barrier, count)
    repeat(1, n_cand, lambda step: send_target(step).start())
    at.each_other_chip(lambda plane, i: send_ids(plane, i).start())
    own_ids.start()
    for i in range(parts):
        swap(i).start()

    for name in ("leaf_ids", "leaf"):
        loads[name].wait()
    trees = leaf_ids.shape[1]
    leaves = leaf_table.shape[0] // trees
    spread_row = lax.broadcasted_iota(jnp.int32, (trees, trees * leaves), 0)
    spread_col = lax.broadcasted_iota(jnp.int32, (trees, trees * leaves), 1)
    spread = (spread_row == spread_col // leaves).astype(F32).astype(BF16)
    wide = jnp.dot(leaf_ids[...].astype(F32).astype(BF16), spread, preferred_element_type=F32)
    leaf_of = lax.broadcasted_iota(jnp.int32, wide.shape, 1) % leaves
    hot = (wide == leaf_of.astype(F32)).astype(F32).astype(BF16)
    leaf_vec = jnp.dot(hot, leaf_table[...], preferred_element_type=F32).astype(BF16)
    repeat(1, EARLY, arrived_group)

    def to_scalar(chip, i):
        return pltpu.make_async_copy(ids_got.at[chip], ids_s.at[i], ids_sem.at[i])

    def fetch(plane, first, last):
        for i in range(first, last):
            chip = at.chip_in(plane, i)
            ids_of(chip).wait_recv()
            to_scalar(chip, i).start()

    in_plane = len(at.steps)
    batch = 4
    fetch(at.plane(0), 0, in_plane)
    for i in range(parts):
        swap(i).wait_recv()
        widen(other, 1 - at.core, i * part, part)

    def one_plane(j):
        plane = at.plane(j)
        for i in range(in_plane):
            chip = at.chip_in(plane, i)
            to_scalar(chip, i).wait()
            for row in range(n_rows):
                row_sum = None
                for slot in range(bag):
                    line = table[pl.ds(ids_s[i, 0, slot * n_rows + row], 1), :]
                    row_sum = line if row_sum is None else row_sum + line
                total[i % 2, pl.ds(row, 1), :] = row_sum
            sums[chip] = total[i % 2].astype(BF16)
            if i > 0:
                send_sums(plane, i - 1).start()
            if i % batch == batch - 1:

                @pl.when(j < at.side - 1)
                def _():
                    fetch(at.plane(j + 1), i - batch + 1, i + 1)
                    if i == in_plane - 1:
                        send_sums(plane, i).start()

    repeat(0, at.side, one_plane)
    got[at.chip] = sums[at.chip]

    repeat(EARLY, n_cand, arrived_group)
    loads["length"].wait()
    length = length_s[0]
    live = lax.broadcasted_iota(jnp.int32, scores.shape, 1) < length
    weights = jnp.where(live, scores[...], 0.0).astype(BF16)
    weighted = jnp.dot(weights, history[...], preferred_element_type=F32)
    root = jnp.sqrt(jnp.full((1, 1), length, jnp.int32).astype(F32))
    weighted = weighted * (1.0 / root)
    interest[...] = weighted.reshape(interest.shape)

    back[at.cand] = interest[at.cand]
    for name in ("rows", "w_first"):
        loads[name].wait()
    table_width = w_first.shape[0] - 3 * width
    hidden_ref[...] = jnp.dot(
        target_rows[...], w_first[pl.ds(table_width + width, width), :], preferred_element_type=F32
    ) + jnp.dot(leaf_vec, w_first[pl.ds(table_width + 2 * width, width), :], preferred_element_type=F32)

    repeat(1, n_cand, lambda step: send_back(step).start())
    for name in ("w_second", "w_third", "w_out"):
        loads[name].wait()

    def add_plane(plane):
        first = pl.multiple_of(plane * at.chips_x, in_plane)
        for t in range(in_plane // halves):
            both = got[first + 2 * t].astype(F32) + got[first + 2 * t + 1].astype(F32)
            pooled[:, pl.ds(t * emb, emb)] = both.astype(BF16)
        depth = in_plane // halves * emb
        rows = pl.ds(pl.multiple_of(lax.div(plane * at.chips_x, halves) * emb, depth), depth)
        hidden_ref[...] += jnp.dot(pooled[...], w_first[rows, :], preferred_element_type=F32)

    def far_plane(j):
        plane = at.plane_from(j)
        for i in range(in_plane):
            sums_of(at.chip_in(plane, i)).wait_recv()
        add_plane(plane)

    repeat(0, at.side - 1, far_plane)
    for i in range(in_plane - 1):
        sums_of(at.chip_in(at.grp - at.ys[0], i)).wait_recv()
    add_plane(at.grp - at.ys[0])
    repeat(1, n_cand, lambda step: back_from(step).wait_recv())
    seen = back[...].reshape(n_rows, width).astype(BF16)
    hidden = hidden_ref[...] + jnp.dot(seen, w_first[pl.ds(table_width, width), :], preferred_element_type=F32)
    one = jnp.maximum(hidden, 0.0).astype(BF16)
    two = jnp.maximum(jnp.dot(one, w_second[...], preferred_element_type=F32), 0.0).astype(BF16)
    three = jnp.maximum(jnp.dot(two, w_third[...], preferred_element_type=F32), 0.0).astype(BF16)
    logit = jnp.sum(three.astype(F32) * w_out[...].astype(F32), axis=1, keepdims=True)
    n_req, per_req = out_ref.shape
    row = lax.broadcasted_iota(jnp.int32, (n_rows, 128), 0) % per_req
    lane = lax.broadcasted_iota(jnp.int32, (n_rows, 128), 1)
    placed = jnp.where(row == lane, logit, 0.0).reshape(n_req, per_req, 128)
    out_ref[...] = jnp.sum(placed, axis=1)[:, :per_req]

    repeat(1, at.chips, lambda step: ids_of(at.chip_after(step)).wait_send())
    repeat(1, n_cand, lambda step: send_target(step).wait_send())
    for i in range(parts):
        swap(i).wait_send()
    repeat(1, n_cand, lambda step: send_back(step).wait_send())
    repeat(1, at.chips, lambda step: sums_of(at.chip_after(step)).wait_send())


def on_device(
    n_grp, n_cand, history, lengths, target, bag_ids, leaf_ids, table_piece, leaf_table,
    w_query, w_key, w_pair, a_out, w_first, w_second, w_third, w_out,
):
    n_req, per_req, width = target.shape
    rows = n_req * per_req
    _, _, tables, bag = bag_ids.shape
    _, piece_rows, emb = table_piece.shape
    _, events, _ = history.shape
    trees, leaves, _ = leaf_table.shape
    att = w_pair.shape[1]
    chips = n_grp * n_cand // 2
    halves = chips // tables
    dma = pltpu.SemaphoreType.DMA
    hbm = pl.BlockSpec(memory_space=pl.ANY)

    args = (
        jnp.transpose(bag_ids, (0, 1, 3, 2)).reshape(rows, bag, tables), lengths, target,
        target.reshape(rows, width), leaf_ids.reshape(rows, trees), history,
        leaf_table.reshape(trees * leaves, width), table_piece, w_query, w_key, w_pair, a_out.reshape(1, att),
        w_first, w_second, w_third, w_out.reshape(1, -1),
    )

    def held(i):
        return pltpu.VMEM(args[i].shape, args[i].dtype)

    return pl.pallas_call(
        functools.partial(kernel, n_grp, n_cand),
        out_shape=jax.ShapeDtypeStruct((n_req, per_req), F32),
        in_specs=[hbm] * len(args),
        out_specs=pl.BlockSpec(memory_space=pltpu.VMEM),
        scratch_shapes=[
            held(0), pltpu.SMEM((1,), jnp.int32), held(2), held(3), held(4), pltpu.VMEM((events, width), BF16),
            held(6), pltpu.VMEM((piece_rows, emb), BF16), held(8), held(9), held(10), held(11),
            held(12), held(13), held(14), held(15),
            pltpu.VMEM((tables, halves, 1, rows * bag), jnp.int32),
            pltpu.VMEM((chips, 1, rows * bag), jnp.int32),
            pltpu.SMEM((chips // math.isqrt(n_grp), 1, rows * bag), jnp.int32),
            pltpu.VMEM((piece_rows, emb), BF16),
            pltpu.VMEM((2 * piece_rows + 8, emb), F32),
            pltpu.VMEM((2, rows, emb), F32),
            pltpu.VMEM((chips, rows, emb), BF16),
            pltpu.VMEM((chips, rows, emb), BF16),
            pltpu.VMEM((n_cand, per_req, width), BF16),
            pltpu.VMEM((n_cand, per_req, width), F32),
            pltpu.VMEM((n_cand, per_req, width), F32),
            pltpu.VMEM((rows, events), F32),
            pltpu.VMEM((per_req * att, width), BF16),
            pltpu.VMEM((rows, tables * emb // math.isqrt(n_grp)), BF16),
            pltpu.VMEM((rows, w_first.shape[1]), F32),
            dma((len(args),)), dma((chips,)), dma((chips,)), dma((chips // math.isqrt(n_grp),)), dma((PARTS,)), dma((PARTS,)),
            dma((n_cand,)), dma((n_cand,)), dma((chips,)), dma((chips,)), dma((n_cand,)), dma((n_cand,)),
        ],
        compiler_params=pltpu.CompilerParams(
            collective_id=0, has_side_effects=True, vmem_limit_bytes=56 * 1024 * 1024
        ),
        name="rank",
    )(*args)


def solution(mesh):
    n_grp, n_cand = mesh.shape["grp"], mesh.shape["cand"]
    both = ("grp", "cand")
    placed = (
        P(both, None, None), P(both), P("grp", "cand", None), P("grp", "cand", None, None),
        P("grp", "cand", None), P(both, None, None),
    ) + (P(),) * 9
    return jax.shard_map(
        functools.partial(on_device, n_grp, n_cand),
        mesh=mesh, in_specs=placed, out_specs=P("grp", "cand"), check_vma=False,
    )
```

```python
import functools
import math

import jax
import jax.numpy as jnp
from jax import lax
from jax.experimental import pallas as pl
from jax.experimental.pallas import tpu as pltpu
from jax.sharding import PartitionSpec as P

MESH = pl.DeviceIdType.MESH
PARTS = 4
EARLY = 3
F32 = jnp.float32
BF16 = jnp.bfloat16


class Place:
    def __init__(self, n_grp, n_cand):
        self.side = math.isqrt(n_grp)
        self.chips_x = n_cand // 2
        self.chips = n_grp * self.chips_x
        self.grp = lax.axis_index("grp")
        self.cand = lax.axis_index("cand")
        self.core = lax.rem(self.cand, 2)
        self.x = lax.div(self.cand, 2)
        self.z = lax.div(self.grp, self.side)
        self.chip = self.grp * self.chips_x + self.x
        y = lax.rem(self.grp, self.side)
        self.ys = [lax.rem(y + dy, self.side) for dy in range(self.side)]
        self.xs = [lax.rem(self.x + dx, self.chips_x) for dx in range(self.chips_x)]
        far_y = sorted(range(self.side), key=lambda d: -min(d, self.side - d))
        far_x = sorted(range(self.chips_x), key=lambda d: -min(d, self.chips_x - d))
        self.steps = [(dy, dx) for dy in far_y for dx in far_x]

    def plane(self, j):
        dz = 2 - j + 3 * (j // 2) - 2 * (j // 3) if isinstance(j, int) else (
            2 - j + 3 * lax.div(j, 2) - 2 * lax.div(j, 3)
        )
        return lax.rem(self.z + dz, self.side) * self.side

    def plane_from(self, j):
        dz = 2 + j - 3 * lax.div(j, 2) + 2 * lax.div(j, 3)
        return lax.rem(self.z + dz, self.side) * self.side

    def chip_in(self, plane, i):
        dy, dx = self.steps[i]
        return (plane + self.ys[dy]) * self.chips_x + self.xs[dx]

    def same_core(self, plane, i):
        dy, dx = self.steps[i]
        return (plane + self.ys[dy], 2 * self.xs[dx] + self.core)

    def other_core(self, step):
        return (self.grp, 2 * self.xs[step] + 1 - self.core)

    def chip_after(self, step):
        return lax.rem(self.chip + step, self.chips)

    def each_other_chip(self, act):
        def far(j):
            plane = self.plane(j)
            for i in range(len(self.steps)):
                act(plane, i)

        repeat(0, self.side - 1, far)
        for i in range(len(self.steps) - 1):
            act(self.grp - self.ys[0], i)

    def enter(self):
        barrier = pltpu.get_barrier_semaphore()
        self.each_other_chip(
            lambda plane, i: pl.semaphore_signal(
                barrier, inc=1, device_id=self.same_core(plane, i), device_id_type=MESH
            )
        )
        for step in range(self.chips_x):
            pl.semaphore_signal(barrier, inc=1, device_id=self.other_core(step), device_id_type=MESH)
        return barrier, self.chips - 1 + self.chips_x


def repeat(first, last, act):
    def body(step, carry):
        act(step)
        return carry

    lax.fori_loop(first, last, body, 0)


def kernel(
    n_grp, n_cand, bag_hbm, length_hbm, target_hbm, rows_hbm, leaf_ids_hbm, history_hbm, leaf_hbm, piece_hbm,
    w_query_hbm, w_key_hbm, w_pair_hbm, a_out_hbm, w_first_hbm, w_second_hbm, w_third_hbm, w_out_hbm,
    out_ref,
    bags, length_s, target, target_rows, leaf_ids, history, leaf_table, own, w_query, w_key, w_pair, a_out,
    w_first, w_second, w_third, w_out,
    ids_stage, ids_got, ids_s, other, table, total, sums, got, cands, back, interest, scores, comb, pooled, hidden_ref,
    load_sem, ids_send, ids_recv, ids_sem, swap_send, swap_recv, t_send, t_recv,
    sum_send, sum_recv, back_send, back_recv,
):
    at = Place(n_grp, n_cand)
    barrier, count = at.enter()
    pairs = dict(
        bags=(bag_hbm, bags), own=(piece_hbm.at[0], own), target=(target_hbm, target),
        w_pair=(w_pair_hbm, w_pair), w_key=(w_key_hbm, w_key), w_query=(w_query_hbm, w_query),
        a_out=(a_out_hbm, a_out), history=(history_hbm.at[0], history), leaf_ids=(leaf_ids_hbm, leaf_ids),
        leaf=(leaf_hbm, leaf_table), rows=(rows_hbm, target_rows), length=(length_hbm, length_s),
        w_first=(w_first_hbm, w_first), w_second=(w_second_hbm, w_second), w_third=(w_third_hbm, w_third),
        w_out=(w_out_hbm, w_out),
    )
    loads = {
        name: pltpu.make_async_copy(src, dst, load_sem.at[i])
        for i, (name, (src, dst)) in enumerate(pairs.items())
    }
    for load in loads.values():
        load.start()

    n_rows, bag, tables = bags.shape
    piece_rows, emb = other.shape
    half_rows = 2 * piece_rows
    halves = at.chips // tables
    parts = PARTS
    part = piece_rows // parts

    loads["bags"].wait()
    turned = [bags[:, slot, :].T for slot in range(bag)]
    for half in range(halves):
        for slot in range(0, bag, 2):
            both = jnp.concatenate(turned[slot : slot + 2], axis=1) - half * half_rows
            both = jnp.where((both >= 0) & (both < half_rows), both, half_rows)
            ids_stage[:, half, 0, pl.ds(slot * n_rows, 2 * n_rows)] = both

    def staged(chip):
        return ids_stage.at[lax.div(chip, halves), lax.rem(chip, halves)]

    def send_ids(plane, i):
        to = at.chip_in(plane, i)
        return pltpu.make_async_remote_copy(
            src_ref=staged(to), dst_ref=ids_got.at[at.chip],
            send_sem=ids_send.at[to], recv_sem=ids_recv.at[at.chip],
            device_id=at.same_core(plane, i), device_id_type=MESH,
        )

    def ids_of(chip):
        return pltpu.make_async_remote_copy(
            src_ref=ids_stage.at[0, 0], dst_ref=ids_got.at[chip],
            send_sem=ids_send.at[chip], recv_sem=ids_recv.at[chip],
            device_id=at.other_core(0), device_id_type=MESH,
        )

    own_ids = pltpu.make_async_copy(staged(at.chip), ids_got.at[at.chip], ids_recv.at[at.chip])

    def send_target(step):
        to = lax.rem(at.cand + step, n_cand)
        return pltpu.make_async_remote_copy(
            src_ref=target.at[to], dst_ref=cands.at[at.cand],
            send_sem=t_send.at[step], recv_sem=t_recv.at[at.cand],
            device_id=(at.grp, to), device_id_type=MESH,
        )

    def target_from(step):
        cand = lax.rem(at.cand + step, n_cand)
        return pltpu.make_async_remote_copy(
            src_ref=target.at[cand], dst_ref=cands.at[cand],
            send_sem=t_send.at[step], recv_sem=t_recv.at[cand],
            device_id=(at.grp, cand), device_id_type=MESH,
        )

    def swap(i):
        rows = pl.ds(i * part, part)
        return pltpu.make_async_remote_copy(
            src_ref=own.at[rows], dst_ref=other.at[rows],
            send_sem=swap_send.at[i], recv_sem=swap_recv.at[i],
            device_id=at.other_core(0), device_id_type=MESH,
        )

    def send_sums(plane, i):
        to = at.chip_in(plane, i)
        return pltpu.make_async_remote_copy(
            src_ref=sums.at[to], dst_ref=got.at[at.chip],
            send_sem=sum_send.at[to], recv_sem=sum_recv.at[at.chip],
            device_id=at.same_core(plane, i), device_id_type=MESH,
        )

    def sums_of(chip):
        return pltpu.make_async_remote_copy(
            src_ref=sums.at[chip], dst_ref=got.at[chip],
            send_sem=sum_send.at[chip], recv_sem=sum_recv.at[chip],
            device_id=at.other_core(0), device_id_type=MESH,
        )

    def send_back(step):
        to = lax.rem(at.cand + step, n_cand)
        return pltpu.make_async_remote_copy(
            src_ref=interest.at[to], dst_ref=back.at[at.cand],
            send_sem=back_send.at[step], recv_sem=back_recv.at[at.cand],
            device_id=(at.grp, to), device_id_type=MESH,
        )

    def back_from(step):
        cand = lax.rem(at.cand + step, n_cand)
        return pltpu.make_async_remote_copy(
            src_ref=interest.at[cand], dst_ref=back.at[cand],
            send_sem=back_send.at[step], recv_sem=back_recv.at[cand],
            device_id=(at.grp, cand), device_id_type=MESH,
        )

    chunk = 512

    def widen(piece, core, first, rows):
        def step(i):
            here = pl.multiple_of(first + i * chunk, chunk)
            there = pl.multiple_of(core * piece_rows + first + i * chunk, chunk)
            table[pl.ds(there, chunk), :] = piece[pl.ds(here, chunk), :].astype(F32)

        repeat(0, rows // chunk, step)

    loads["own"].wait()
    widen(own, at.core, 0, piece_rows)
    table[pl.ds(half_rows, 8), :] = jnp.zeros((8, emb), F32)
    loads["target"].wait()
    cands[at.cand] = target[at.cand]
    for name in ("w_pair", "w_key", "w_query", "a_out", "history"):
        loads[name].wait()
    events, width = history.shape
    att = w_pair.shape[1]
    per_src = cands.shape[1]
    pair_t = w_pair[...].astype(F32).T
    key_t = w_key[...].astype(F32).T
    query_t = w_query[...].astype(F32).T.astype(BF16)
    a_col = a_out[...].astype(F32).T
    a_wide = jnp.broadcast_to(a_col, (att, 256))
    history_t = history[...].astype(F32).T.astype(BF16)

    def one_group(step):
        g = lax.rem(at.cand + step, n_cand)
        rows_f = cands[g].astype(F32)
        q_part = lax.dot_general(query_t, cands[g], (((1,), (1,)), ((), ())), preferred_element_type=F32)
        base = jnp.sum(q_part * a_col, axis=0, keepdims=True)
        for c in range(per_src):
            comb[pl.ds(c * att, att), :] = (rows_f[c : c + 1, :] * pair_t + key_t).astype(BF16)
        for block in range(events // 256):
            cols = pl.ds(block * 256, 256)
            raw = jnp.dot(comb[...], history_t[:, block * 256 : block * 256 + 256], preferred_element_type=F32)
            for c in range(per_src):
                unit = jnp.maximum(raw[c * att : (c + 1) * att, :], -q_part[:, c : c + 1]) * a_wide
                line = jnp.sum(unit, axis=0, keepdims=True) + base[:, c : c + 1]
                scores[pl.ds(g * per_src + c, 1), cols] = line

    def arrived_group(step):
        target_from(step).wait_recv()
        one_group(step)

    one_group(0)

    for name in ("leaf_ids", "leaf"):
        loads[name].wait()
    trees = leaf_ids.shape[1]
    leaves = leaf_table.shape[0] // trees
    spread_row = lax.broadcasted_iota(jnp.int32, (trees, trees * leaves), 0)
    spread_col = lax.broadcasted_iota(jnp.int32, (trees, trees * leaves), 1)
    spread = (spread_row == spread_col // leaves).astype(F32).astype(BF16)
    wide = jnp.dot(leaf_ids[...].astype(F32).astype(BF16), spread, preferred_element_type=F32)
    leaf_of = lax.broadcasted_iota(jnp.int32, wide.shape, 1) % leaves
    hot = (wide == leaf_of.astype(F32)).astype(F32).astype(BF16)
    leaf_vec = jnp.dot(hot, leaf_table[...], preferred_element_type=F32).astype(BF16)
    for name in ("rows", "w_first"):
        loads[name].wait()
    table_width = w_first.shape[0] - 3 * width
    hidden_ref[...] = jnp.dot(
        target_rows[...], w_first[pl.ds(table_width + width, width), :], preferred_element_type=F32
    ) + jnp.dot(leaf_vec, w_first[pl.ds(table_width + 2 * width, width), :], preferred_element_type=F32)

    pl.semaphore_wait(barrier, count)
    repeat(1, n_cand, lambda step: send_target(step).start())
    at.each_other_chip(lambda plane, i: send_ids(plane, i).start())
    own_ids.start()
    for i in range(parts):
        swap(i).start()

    repeat(1, EARLY, arrived_group)

    def to_scalar(chip, i):
        return pltpu.make_async_copy(ids_got.at[chip], ids_s.at[i], ids_sem.at[i])

    def fetch(plane, first, last):
        for i in range(first, last):
            chip = at.chip_in(plane, i)
            ids_of(chip).wait_recv()
            to_scalar(chip, i).start()

    in_plane = len(at.steps)
    batch = 4
    fetch(at.plane(0), 0, in_plane)
    for i in range(parts):
        swap(i).wait_recv()
        widen(other, 1 - at.core, i * part, part)

    def one_plane(j):
        plane = at.plane(j)
        for i in range(in_plane):
            chip = at.chip_in(plane, i)
            to_scalar(chip, i).wait()
            for row in range(n_rows):
                row_sum = None
                for slot in range(bag):
                    line = table[pl.ds(ids_s[i, 0, slot * n_rows + row], 1), :]
                    row_sum = line if row_sum is None else row_sum + line
                total[i % 2, pl.ds(row, 1), :] = row_sum
            sums[chip] = total[i % 2].astype(BF16)
            if i > 0:
                send_sums(plane, i - 1).start()
            if i % batch == batch - 1:

                @pl.when(j < at.side - 1)
                def _():
                    fetch(at.plane(j + 1), i - batch + 1, i + 1)
                    if i == in_plane - 1:
                        send_sums(plane, i).start()

    repeat(0, at.side, one_plane)
    got[at.chip] = sums[at.chip]

    repeat(EARLY, n_cand, arrived_group)
    loads["length"].wait()
    length = length_s[0]
    live = lax.broadcasted_iota(jnp.int32, scores.shape, 1) < length
    weights = jnp.where(live, scores[...], 0.0).astype(BF16)
    weighted = jnp.dot(weights, history[...], preferred_element_type=F32)
    root = jnp.sqrt(jnp.full((1, 1), length, jnp.int32).astype(F32))
    weighted = weighted * (1.0 / root)
    interest[...] = weighted.reshape(interest.shape)

    back[at.cand] = interest[at.cand]
    repeat(1, n_cand, lambda step: send_back(step).start())
    for name in ("w_second", "w_third", "w_out"):
        loads[name].wait()

    def add_plane(plane):
        first = pl.multiple_of(plane * at.chips_x, in_plane)
        for t in range(in_plane // halves):
            both = got[first + 2 * t].astype(F32) + got[first + 2 * t + 1].astype(F32)
            pooled[:, pl.ds(t * emb, emb)] = both.astype(BF16)
        depth = in_plane // halves * emb
        rows = pl.ds(pl.multiple_of(lax.div(plane * at.chips_x, halves) * emb, depth), depth)
        hidden_ref[...] += jnp.dot(pooled[...], w_first[rows, :], preferred_element_type=F32)

    def far_plane(j):
        plane = at.plane_from(j)
        for i in range(in_plane):
            sums_of(at.chip_in(plane, i)).wait_recv()
        add_plane(plane)

    repeat(0, at.side - 1, far_plane)
    for i in range(in_plane - 1):
        sums_of(at.chip_in(at.grp - at.ys[0], i)).wait_recv()
    add_plane(at.grp - at.ys[0])
    repeat(1, n_cand, lambda step: back_from(step).wait_recv())
    seen = back[...].reshape(n_rows, width).astype(BF16)
    hidden = hidden_ref[...] + jnp.dot(seen, w_first[pl.ds(table_width, width), :], preferred_element_type=F32)
    one = jnp.maximum(hidden, 0.0).astype(BF16)
    two = jnp.maximum(jnp.dot(one, w_second[...], preferred_element_type=F32), 0.0).astype(BF16)
    three = jnp.maximum(jnp.dot(two, w_third[...], preferred_element_type=F32), 0.0).astype(BF16)
    logit = jnp.sum(three.astype(F32) * w_out[...].astype(F32).reshape(1, -1), axis=1, keepdims=True)
    n_req, per_req = out_ref.shape
    row = lax.broadcasted_iota(jnp.int32, (n_rows, 128), 0) % per_req
    lane = lax.broadcasted_iota(jnp.int32, (n_rows, 128), 1)
    placed = jnp.where(row == lane, logit, 0.0).reshape(n_req, per_req, 128)
    out_ref[...] = jnp.sum(placed, axis=1)[:, :per_req]

    repeat(1, at.chips, lambda step: ids_of(at.chip_after(step)).wait_send())
    repeat(1, n_cand, lambda step: send_target(step).wait_send())
    for i in range(parts):
        swap(i).wait_send()
    repeat(1, n_cand, lambda step: send_back(step).wait_send())
    repeat(1, at.chips, lambda step: sums_of(at.chip_after(step)).wait_send())


def on_device(
    n_grp, n_cand, history, lengths, target, bag_ids, leaf_ids, table_piece, leaf_table,
    w_query, w_key, w_pair, a_out, w_first, w_second, w_third, w_out,
):
    n_req, per_req, width = target.shape
    rows = n_req * per_req
    _, _, tables, bag = bag_ids.shape
    _, piece_rows, emb = table_piece.shape
    _, events, _ = history.shape
    trees, leaves, _ = leaf_table.shape
    att = w_pair.shape[1]
    chips = n_grp * n_cand // 2
    halves = chips // tables
    dma = pltpu.SemaphoreType.DMA
    hbm = pl.BlockSpec(memory_space=pl.ANY)

    args = (
        jnp.transpose(bag_ids, (0, 1, 3, 2)).reshape(rows, bag, tables), lengths, target,
        target.reshape(rows, width), leaf_ids.reshape(rows, trees), history,
        leaf_table.reshape(trees * leaves, width), table_piece, w_query, w_key, w_pair, a_out.reshape(1, att),
        w_first, w_second, w_third, w_out,
    )

    def held(i):
        return pltpu.VMEM(args[i].shape, args[i].dtype)

    return pl.pallas_call(
        functools.partial(kernel, n_grp, n_cand),
        out_shape=jax.ShapeDtypeStruct((n_req, per_req), F32),
        in_specs=[hbm] * len(args),
        out_specs=pl.BlockSpec(memory_space=pltpu.VMEM),
        scratch_shapes=[
            held(0), pltpu.SMEM((1,), jnp.int32), held(2), held(3), held(4), pltpu.VMEM((events, width), BF16),
            held(6), pltpu.VMEM((piece_rows, emb), BF16), held(8), held(9), held(10), held(11),
            held(12), held(13), held(14), held(15),
            pltpu.VMEM((tables, halves, 1, rows * bag), jnp.int32),
            pltpu.VMEM((chips, 1, rows * bag), jnp.int32),
            pltpu.SMEM((chips // math.isqrt(n_grp), 1, rows * bag), jnp.int32),
            pltpu.VMEM((piece_rows, emb), BF16),
            pltpu.VMEM((2 * piece_rows + 8, emb), F32),
            pltpu.VMEM((2, rows, emb), F32),
            pltpu.VMEM((chips, rows, emb), BF16),
            pltpu.VMEM((chips, rows, emb), BF16),
            pltpu.VMEM((n_cand, per_req, width), BF16),
            pltpu.VMEM((n_cand, per_req, width), F32),
            pltpu.VMEM((n_cand, per_req, width), F32),
            pltpu.VMEM((rows, events), F32),
            pltpu.VMEM((per_req * att, width), BF16),
            pltpu.VMEM((rows, tables * emb // math.isqrt(n_grp)), BF16),
            pltpu.VMEM((rows, w_first.shape[1]), F32),
            dma((len(args),)), dma((chips,)), dma((chips,)), dma((chips // math.isqrt(n_grp),)), dma((PARTS,)), dma((PARTS,)),
            dma((n_cand,)), dma((n_cand,)), dma((chips,)), dma((chips,)), dma((n_cand,)), dma((n_cand,)),
        ],
        compiler_params=pltpu.CompilerParams(
            collective_id=0, has_side_effects=True, vmem_limit_bytes=56 * 1024 * 1024
        ),
        name="rank",
    )(*args)


def solution(mesh):
    n_grp, n_cand = mesh.shape["grp"], mesh.shape["cand"]
    both = ("grp", "cand")
    placed = (
        P(both, None, None), P(both), P("grp", "cand", None), P("grp", "cand", None, None),
        P("grp", "cand", None), P(both, None, None),
    ) + (P(),) * 9
    return jax.shard_map(
        functools.partial(on_device, n_grp, n_cand),
        mesh=mesh, in_specs=placed, out_specs=P("grp", "cand"), check_vma=False,
    )
```
